1024 devices in a mesh: fsdp: 16 (over y, z_hi), sample: 8 (over x, core), tp: 8 (over z_lo).
Axes of the slice: x: 4, y: 4, z: 32 (z_hi: 4, z_lo: 8; z = z_hi * 8 + z_lo), core: 2. Of those that a mesh axis runs over, the one named last changes fastest.
Arguments:
- hidden: bfloat16 [32, 128, 4, 4096], P('fsdp', 'sample'), may hold values from -6 to 6
- qkv_weight: bfloat16 [4096, 8, 768], P('fsdp', 'tp'), may hold values from -0.09375 to 0.09375
- qkv_bias: float32 [8, 768], P('tp'), may hold values from -6 to 6
- prompt_pool: bfloat16 [32, 48, 16, 8, 256], P('fsdp', 'sample', None, 'tp'), as said below
- block_table: int32 [32, 32], P('fsdp', 'sample'), may hold values from 0 to 5, as said below
- group_prompts: int32 [32], P('fsdp'), may hold values from 0 to 31, each once
- decode_len: int32 [32, 128], P('fsdp', 'sample'), may hold values from 1 to 4
Outputs:
- attn_out: bfloat16 [32, 128, 4, 8, 512], P('fsdp', 'sample', None, 'tp')
The draws below stay inside these ranges and needn't reach their ends.
Inputs may be any that keep to these rules, and one draw needn't show every extreme that they name: `block_table`: for each prompt and each sample index s, the 4 entries in columns s * 4 to (s + 1) * 4 - 1 are distinct. `group_prompts`: each prompt is named by exactly one slot. `prompt_pool`: keys already carry their positions' rotation.
All inputs are finite; a program needn't handle non-finite values.
Results may differ from the reference program's by a relative error of at most 0.012.
Values may be sent and summed in bfloat16 or wider, within the bound.
No kernel may reach another device: no remote copies, remote signals or barrier semaphores. Data moves between devices by JAX's collectives and lax.ppermute only.
A program may use at most 32 MiB of HBM per device.

```python
import jax
import jax.numpy as jnp
from jax import lax

D = 4096
HEADS = 32
KV_HEADS = 8
HD = 128
STEPS = 4
BLK = 16
PBLK_DEV = 4
POOL_DEV = 6
PROMPTS = 32
SAMPLES = 128
PBLK = 32
POOL = 48
PLEN = 512
N_SAMPLE = 8


def draw_prompt_pool(key, part):
    shape_all = (PROMPTS, POOL, BLK, KV_HEADS, 2 * HD)
    key_base = jax.random.fold_in(key, 0)
    return jax.random.normal(key_base, shape_all, jnp.float32).astype(jnp.bfloat16)


def draw_block_table(key, part):
    scores = jax.random.randint(key, (PROMPTS, N_SAMPLE, POOL_DEV), 0, 1 << 20) * POOL_DEV + jnp.arange(POOL_DEV)[None, None, :]
    ordering = jnp.argsort(scores, axis=-1)
    return ordering[..., :PBLK_DEV].reshape(PROMPTS, N_SAMPLE * PBLK_DEV).astype(jnp.int32)


def draw_decode_len(key, part):
    lengths = jax.random.randint(key, (PROMPTS, SAMPLES), 1, STEPS + 1)
    return lengths.at[0, 0].set(STEPS).at[0, 1].set(1).astype(jnp.int32)


def block_levels(own_key, shape, shards, smallest, high):
    level = 1.0
    for position, blocks in shards:
        heights = jax.random.uniform(jax.random.fold_in(jax.random.fold_in(own_key, 6), position), (blocks,), jnp.float32, smallest / len(shards), high / len(shards))
        level = level * jnp.repeat(jnp.exp(heights), shape[position] // blocks).reshape((-1,) + (1,) * (len(shape) - 1 - position))
    return level


def gaussian(own_key, dims, deviation, limit, cuts=(), held_as=jnp.bfloat16):
    loudness = block_levels(own_key, dims, cuts, -0.22, 0.18) if cuts else 1.0
    values = jax.random.normal(own_key, dims, jnp.float32) * deviation * loudness
    return jnp.minimum(jnp.maximum(values, -limit), limit).astype(held_as)


def setup_inputs(seed: int = 0) -> dict:
    splits = jax.random.split(jax.random.key(seed), 8)
    hidden = gaussian(splits[0], (PROMPTS, SAMPLES, STEPS, D), 1.0, 6.0, ((0, 16), (1, 8)))
    qkv_weight = gaussian(splits[1], (D, KV_HEADS, (HEADS // KV_HEADS + 2) * HD), D ** -0.5, 0.09375, ((0, 16), (1, 8)))
    qkv_bias = gaussian(splits[2], (KV_HEADS, (HEADS // KV_HEADS + 2) * HD), 1.0, 6.0, ((0, 8),), jnp.float32)
    prompt_pool = draw_prompt_pool(jax.random.fold_in(splits[7], 71), 0)
    block_table = draw_block_table(jax.random.fold_in(splits[7], 71), 0)
    group_prompts = jax.random.permutation(splits[5], PROMPTS).astype(jnp.int32)
    decode_len = draw_decode_len(jax.random.fold_in(splits[7], 71), 0)
    return dict(hidden=hidden, qkv_weight=qkv_weight, qkv_bias=qkv_bias, prompt_pool=prompt_pool, block_table=block_table, group_prompts=group_prompts, decode_len=decode_len)


def rotate(field, offset):
    step_count = field.shape[2]
    half_dim = field.shape[-1] // 2
    inverse = 1000000.0 ** (-2.0 * jnp.arange(half_dim, dtype=jnp.float32) / field.shape[-1])
    angles = (offset + jnp.arange(step_count, dtype=jnp.float32))[:, None] * inverse[None, :]
    bcast_shape = [1] * field.ndim
    bcast_shape[2] = step_count
    bcast_shape[-1] = half_dim
    cosine = jnp.cos(angles).reshape(bcast_shape)
    sine_part = jnp.sin(angles).reshape(bcast_shape)
    low_half = field[..., :half_dim]
    high_half = field[..., half_dim:]
    return jnp.concatenate([low_half * cosine - high_half * sine_part, high_half * cosine + low_half * sine_part], axis=-1)


def attend(queries, new_keys, new_values, cached_keys, cached_values, lengths):
    scaling = queries.shape[-1] ** -0.5
    prompt_scores = jnp.einsum("psthgd,pnhd->psthgn", queries.astype(jnp.float32), cached_keys.astype(jnp.float32)) * scaling
    own_scores = jnp.einsum("psthgd,psuhd->psthgu", queries.astype(jnp.float32), new_keys.astype(jnp.float32)) * scaling
    step_count = queries.shape[2]
    causal = (jnp.arange(step_count)[None, :] <= jnp.arange(step_count)[:, None]).reshape(1, 1, step_count, 1, 1, step_count)
    own_scores = jnp.where(causal, own_scores, -jnp.inf)
    row_max = jnp.maximum(jnp.max(prompt_scores, axis=-1), jnp.max(own_scores, axis=-1))
    prompt_exp = jnp.exp(prompt_scores - row_max[..., None])
    own_exp = jnp.exp(own_scores - row_max[..., None])
    row_total = jnp.sum(prompt_exp, axis=-1) + jnp.sum(own_exp, axis=-1)
    prompt_w = prompt_exp.astype(jnp.bfloat16).astype(jnp.float32)
    own_w = own_exp.astype(jnp.bfloat16).astype(jnp.float32)
    output = jnp.einsum("psthgn,pnhd->psthgd", prompt_w, cached_values.astype(jnp.float32))
    output = output + jnp.einsum("psthgu,psuhd->psthgd", own_w, new_values.astype(jnp.float32))
    output = output / row_total[..., None]
    live_mask = jnp.arange(step_count)[None, None, :] < lengths[:, :, None]
    output = jnp.where(live_mask[..., None, None, None], output, 0.0)
    shape_out = output.shape
    return output.reshape(shape_out[0], shape_out[1], shape_out[2], shape_out[3], shape_out[4] * shape_out[5]).astype(jnp.bfloat16)


def reference(hidden, qkv_weight, qkv_bias, prompt_pool, block_table, group_prompts, decode_len):
    group_size = HEADS // KV_HEADS
    slot_base = (jnp.arange(PBLK, dtype=jnp.int32) // PBLK_DEV) * POOL_DEV
    physical = (block_table + slot_base[None, :]).astype(jnp.int32)
    weight_flat = qkv_weight.reshape(D, -1)

    def per_slot(index):
        prompt_id = group_prompts[index].astype(jnp.int32)
        pool_rows = lax.dynamic_index_in_dim(prompt_pool, prompt_id, 0, keepdims=False)
        slot_ids = lax.dynamic_index_in_dim(physical, prompt_id, 0, keepdims=False)
        cache = jnp.take(pool_rows, slot_ids, axis=0).reshape(PLEN, KV_HEADS, 2 * HD)
        tokens = lax.dynamic_index_in_dim(hidden, index, 0, keepdims=False).reshape(SAMPLES * STEPS, D)
        mixed = jnp.dot(tokens, weight_flat, preferred_element_type=jnp.float32)
        mixed = mixed.reshape(1, SAMPLES, STEPS, KV_HEADS, (group_size + 2) * HD) + qkv_bias
        queries = mixed[..., :group_size * HD].reshape(1, SAMPLES, STEPS, KV_HEADS, group_size, HD)
        queries = rotate(queries, PLEN).astype(jnp.bfloat16)
        new_keys = rotate(mixed[..., group_size * HD:(group_size + 1) * HD], PLEN).astype(jnp.bfloat16)
        new_values = mixed[..., (group_size + 1) * HD:].astype(jnp.bfloat16)
        lengths = lax.dynamic_index_in_dim(decode_len, index, 0, keepdims=True)
        result = attend(queries, new_keys, new_values, cache[None, :, :, :HD], cache[None, :, :, HD:], lengths)
        return result[0]

    return lax.map(per_slot, jnp.arange(PROMPTS, dtype=jnp.int32))
```

```python
import functools

import jax
import jax.numpy as jnp
import numpy as np
from jax import lax
from jax.experimental import pallas as pl
from jax.experimental.pallas import tpu as pltpu
from jax.sharding import Mesh, PartitionSpec as P

HD = 128
HEADS = 6
GROUP = 4
NY, NZ, NX, NC = 4, 4, 4, 2
SLOTS = 2
SAMPLES_DEV = 16
STEPS = 4
ROWS = SLOTS * SAMPLES_DEV * STEPS
WIDTH = 4096
K_SHARD = 256
W_ROWS = HEADS * HD // NX
TOK = 64
C_ROWS = 2 * TOK
Z_ROWS = W_ROWS + SLOTS * C_ROWS
Y_ROWS = NZ * W_ROWS + SLOTS * C_ROWS
X_ROWS = W_ROWS + NC * SLOTS * C_ROWS
PLEN = 512
INTERPRET = False


def vmem():
    return pl.BlockSpec(memory_space=pltpu.VMEM)


def smem():
    return pl.BlockSpec(memory_space=pltpu.SMEM)


def prep_kernel(place, table, w_ref, pool_ref, out_ref):
    x, c = place[0], place[1]
    wt = w_ref[pl.ds(pl.multiple_of(c * 128, 128), 128), :].T
    for g in range(HEADS * 2):
        for k in range(NX):

            @pl.when(x == k)
            def _(g=g, k=k):
                lo = g * 64 + k * 16
                out_ref[g * 16 : (g + 1) * 16, :] = wt[lo : lo + 16, :]

    for i in range(SLOTS):
        for b in range(4):
            block = pool_ref[i, table[i, b]]
            base = W_ROWS + i * C_ROWS + b * 16
            out_ref[base : base + 16, :] = block[:, :HD]
            out_ref[base + TOK : base + TOK + 16, :] = block[:, HD:]


def pick_kernel(wanted, zg_ref, out_ref):
    for d in range(NY):
        for z in range(NZ):
            out_ref[d, z * W_ROWS : (z + 1) * W_ROWS, :] = zg_ref[z, :W_ROWS, :]
        for i in range(SLOTS):
            p = wanted[d, i] & 7
            src = pl.ds(pl.multiple_of(W_ROWS + (p & 1) * C_ROWS, 64), C_ROWS)
            base = NZ * W_ROWS + i * C_ROWS
            out_ref[d, base : base + C_ROWS, :] = zg_ref[p >> 1, src, :]


def project_kernel(
    place, mine, a_ref, b_ref, h0, h1, h2, h3, bias_ref, cos_ref, sin_ref, out_ref, wt_ref
):
    x, c = place[0], place[1]
    for ref, half in ((a_ref, c), (b_ref, 1 - c)):
        for y in range(NY):
            for z in range(NZ):
                lanes = pl.ds(pl.multiple_of(((y * NZ + z) * 2 + half) * 128, 128), 128)
                wt_ref[:, lanes] = ref[y, z * W_ROWS : (z + 1) * W_ROWS, :]
    at = pl.ds(pl.multiple_of(x * 16, 16), 16)
    cosine = cos_ref[at, :]
    sine = sin_ref[at, :]
    for h_ref, shift in ((h0, 0), (h1, 3), (h2, 1), (h3, 2)):
        mixed = lax.dot_general(
            wt_ref[...], h_ref[...], (((1,), (1,)), ((), ())), preferred_element_type=jnp.float32
        )
        mixed = mixed + bias_ref[...]
        to = (x + shift) & 3
        for g in range(HEADS):
            lo = mixed[g * 32 : g * 32 + 16]
            hi = mixed[g * 32 + 16 : g * 32 + 32]
            if g < GROUP + 1:
                lo, hi = lo * cosine - hi * sine, hi * cosine + lo * sine
            out_ref[to, g * 32 : g * 32 + 16, :] = lo.astype(jnp.bfloat16)
            out_ref[to, g * 32 + 16 : g * 32 + 32, :] = hi.astype(jnp.bfloat16)
    for k, ref in enumerate((a_ref, b_ref)):
        for i in range(SLOTS):
            base = NZ * W_ROWS + i * C_ROWS
            rows = ref[mine[i] >> 3, base : base + C_ROWS, :]
            to = W_ROWS + (k * SLOTS + i) * C_ROWS
            for d in range(NX):
                out_ref[d, to : to + C_ROWS, :] = rows


def attend_kernel(g_ref, live_ref, out_ref, q_ref, kn_ref, vn_ref, kc_ref, vc_ref):
    for x in range(NX):
        for g in range(HEADS):
            for half in range(2):
                rows = g_ref[x, g * 32 + half * 16 : g * 32 + half * 16 + 16, :]
                at = slice(half * 64 + x * 16, half * 64 + x * 16 + 16)
                if g < GROUP:
                    q_ref[at, g * 128 : (g + 1) * 128] = rows
                elif g == GROUP:
                    kn_ref[at, :] = rows
                else:
                    vn_ref[at, :] = rows
        for k in range(NC):
            for i in range(SLOTS):
                base = W_ROWS + (k * SLOTS + i) * C_ROWS
                at = slice((x * NC + k) * TOK, (x * NC + k + 1) * TOK)
                kc_ref[i, at, :] = g_ref[x, base : base + TOK, :]
                vc_ref[i, at, :] = g_ref[x, base + TOK : base + 2 * TOK, :]
    q = q_ref[...]
    scaling = HD ** (-0.5)
    lane = lax.broadcasted_iota(jnp.int32, (1, GROUP * ROWS), 1) & (ROWS - 1)
    second = lane >= ROWS // 2

    def plain(a, b):
        return jnp.dot(a, b, preferred_element_type=jnp.float32)

    def turned(a, b):
        return lax.dot_general(a, b, (((0,), (0,)), ((), ())), preferred_element_type=jnp.float32)

    scores = jnp.where(second, plain(kc_ref[1], q), plain(kc_ref[0], q)) * scaling
    own = turned(kn_ref[...], q) * scaling
    token = lax.broadcasted_iota(jnp.int32, (ROWS, GROUP * ROWS), 0)
    seen = ((token >> 2) == (lane >> 2)) & ((token & 3) <= (lane & 3))
    own = jnp.where(seen, own, -jnp.inf)
    row_max = jnp.maximum(
        jnp.max(scores, axis=0, keepdims=True), jnp.max(own, axis=0, keepdims=True)
    )
    prompt_exp = jnp.exp(scores - row_max)
    own_exp = jnp.exp(own - row_max)
    total = jnp.sum(prompt_exp, axis=0, keepdims=True) + jnp.sum(own_exp, axis=0, keepdims=True)
    weights = prompt_exp.astype(jnp.bfloat16)
    out = jnp.where(second, turned(vc_ref[1], weights), turned(vc_ref[0], weights))
    out = out + plain(vn_ref[...], own_exp.astype(jnp.bfloat16))
    out = out / total
    for h in range(GROUP):
        part = out[:, h * 128 : (h + 1) * 128]
        part = jnp.where(live_ref[...] > 0, part, 0.0)
        out_ref[:, h * 128 : (h + 1) * 128] = part.T.astype(jnp.bfloat16)


def tables():
    inverse = 1000000.0 ** (-2.0 * np.arange(64) / HD)
    step = np.arange(ROWS) % STEPS
    angles = (PLEN + step)[None, :] * inverse[:, None]
    return np.cos(angles).astype(np.float32), np.sin(angles).astype(np.float32)


def call(kernel, shape, specs, dtype=jnp.bfloat16, scratch=(), flops=0, moved=0):
    return pl.pallas_call(
        kernel,
        out_shape=jax.ShapeDtypeStruct(shape, dtype),
        in_specs=specs,
        out_specs=vmem(),
        scratch_shapes=list(scratch),
        cost_estimate=pl.CostEstimate(flops=flops, bytes_accessed=moved, transcendentals=0),
        interpret=INTERPRET,
    )


def hop(array, axis, size, by):
    return lax.ppermute(array, axis, [(i, (i + by) % size) for i in range(size)])


def body(hidden, qkv_weight, qkv_bias, prompt_pool, block_table, group_prompts, decode_len):
    bf16 = jnp.bfloat16
    x = lax.axis_index("x").astype(jnp.int32)
    c = lax.axis_index("c").astype(jnp.int32)
    place = jnp.stack([x, c])

    h0 = hidden.reshape(ROWS, WIDTH)
    h1 = hop(h0, "x", NX, 1)
    h2 = hop(h0, "x", NX, -1)
    h3 = hop(h0, "x", NX, 2)

    wanted = lax.all_gather(group_prompts, "y", axis=0, tiled=False)
    sent = call(
        prep_kernel, (Z_ROWS, 128), [smem(), smem(), vmem(), vmem()], moved=600000
    )(
        place,
        block_table,
        qkv_weight.reshape(K_SHARD, HEADS * HD),
        prompt_pool.reshape(SLOTS, 6, 16, 2 * HD),
    )
    zg = lax.all_gather(sent, "zh", axis=0, tiled=True).reshape(NZ, Z_ROWS, 128)
    picked = call(pick_kernel, (NY, Y_ROWS, 128), [smem(), vmem()], moved=1500000)(wanted, zg)
    a = lax.all_to_all(picked, "y", 0, 0, tiled=True)
    b = hop(a, "c", NC, 1)

    bias = lax.dynamic_slice_in_dim(qkv_bias.reshape(HEADS * 2, NX, 16), x, 1, axis=1)
    bias = jnp.broadcast_to(bias.reshape(W_ROWS, 1), (W_ROWS, ROWS))
    cosine, sine = tables()
    made = call(
        project_kernel,
        (NX, X_ROWS, 128),
        [smem(), smem()] + [vmem()] * 9,
        scratch=[pltpu.VMEM((W_ROWS, WIDTH), bf16)],
        flops=2 * W_ROWS * WIDTH * 4 * ROWS,
        moved=7000000,
    )(place, group_prompts, a, b, h0, h1, h2, h3, bias, jnp.asarray(cosine), jnp.asarray(sine))
    got = lax.all_to_all(made, "x", 0, 0, tiled=True)

    step = jnp.arange(STEPS, dtype=jnp.int32)
    live = (step[None, None, :] < decode_len[:, :, None]).astype(jnp.float32).reshape(1, ROWS)
    out = call(
        attend_kernel,
        (ROWS, GROUP * HD),
        [vmem(), vmem()],
        scratch=[
            pltpu.VMEM((HD, GROUP * ROWS), bf16),
            pltpu.VMEM((HD, ROWS), bf16),
            pltpu.VMEM((HD, ROWS), bf16),
            pltpu.VMEM((SLOTS, PLEN, HD), bf16),
            pltpu.VMEM((SLOTS, PLEN, HD), bf16),
        ],
        flops=400000000,
        moved=1000000,
    )(got, live)
    return out.reshape(SLOTS, SAMPLES_DEV, STEPS, 1, GROUP * HD)


def solution(mesh):
    names = ("y", "zh", "x", "c", "tp")
    fine = Mesh(mesh.devices.reshape(NY, NZ, NX, NC, mesh.shape["tp"]), names)
    fsdp, sample = ("y", "zh"), ("x", "c")
    return jax.shard_map(
        body,
        mesh=fine,
        in_specs=(
            P(fsdp, sample, None, None),
            P(fsdp, "tp", None),
            P("tp", None),
            P(fsdp, sample, None, "tp", None),
            P(fsdp, sample),
            P(fsdp),
            P(fsdp, sample),
        ),
        out_specs=P(fsdp, sample, None, "tp", None),
        check_vma=False,
    )
```

```python
import jax
import jax.numpy as jnp
import numpy as np
from jax import lax
from jax.experimental import pallas as pl
from jax.experimental.pallas import tpu as pltpu
from jax.sharding import Mesh, PartitionSpec as P


HD = 128
HEADS = 6
GROUP = 4
NY, NZ, NX, NC = 4, 4, 4, 2
SLOTS = 2
SAMPLES_DEV = 16
STEPS = 4
ROWS = SLOTS * SAMPLES_DEV * STEPS
WIDTH = 4096
K_SHARD = 256
W_ROWS = HEADS * HD // (NX * NC)
TOK = 64
C_ROWS = 2 * TOK
Z_ROWS = 2 * W_ROWS + SLOTS * C_ROWS
Y_ROWS = NZ * 2 * W_ROWS + SLOTS * C_ROWS
X_ROWS = W_ROWS + SLOTS * C_ROWS
PLEN = 512
INTERPRET = False


def vmem():
    return pl.BlockSpec(memory_space=pltpu.VMEM)


def smem():
    return pl.BlockSpec(memory_space=pltpu.SMEM)


def prep_kernel(place, table, w_ref, pool_ref, out_ref):
    wt = w_ref[...].T
    for k in range(NX * NC):

        @pl.when(place[0] * NC + place[1] == k)
        def _(k=k):
            for g in range(HEADS * 2):
                lo = g * 64 + k * 8
                for half in range(2):
                    out_ref[half * W_ROWS + g * 8 : half * W_ROWS + (g + 1) * 8, :] = wt[
                        lo : lo + 8, half * 128 : (half + 1) * 128
                    ]

    for i in range(SLOTS):
        for b in range(4):
            block = pool_ref[i, table[i, b]]
            base = 2 * W_ROWS + i * C_ROWS + b * 16
            out_ref[base : base + 16, :] = block[:, :HD]
            out_ref[base + TOK : base + TOK + 16, :] = block[:, HD:]


def pick_kernel(wanted, zg_ref, out_ref):
    for d in range(NY):
        for z in range(NZ):
            out_ref[d, z * 2 * W_ROWS : (z + 1) * 2 * W_ROWS, :] = zg_ref[z, : 2 * W_ROWS, :]
        for i in range(SLOTS):
            p = wanted[d, i] & 7
            src = pl.ds(pl.multiple_of(2 * W_ROWS + (p & 1) * C_ROWS, 64), C_ROWS)
            base = NZ * 2 * W_ROWS + i * C_ROWS
            out_ref[d, base : base + C_ROWS, :] = zg_ref[p >> 1, src, :]


def project(place, core, mine, from_ref, h_refs, bias_ref, cos_ref, sin_ref, wt_ref, put):
    for y in range(NY):
        for z in range(NZ):
            for half in range(2):
                lo = ((y * NZ + z) * 2 + half) * 128
                wt_ref[:, lo : lo + 128] = from_ref[
                    y, (z * 2 + half) * W_ROWS : (z * 2 + half + 1) * W_ROWS, :
                ]
    at = pl.ds(pl.multiple_of(place[0] * 16 + core * 8, 8), 8)
    cosine = cos_ref[at, :]
    sine = sin_ref[at, :]
    bias = bias_ref[core]
    for h_ref, shift in zip(h_refs, (0, 3, 1, 2)):
        mixed = lax.dot_general(
            wt_ref[...], h_ref[...], (((1,), (1,)), ((), ())), preferred_element_type=jnp.float32
        )
        mixed = mixed + bias
        to = (place[0] + shift) & 3
        for g in range(HEADS):
            lo = mixed[g * 16 : g * 16 + 8]
            hi = mixed[g * 16 + 8 : g * 16 + 16]
            if g < GROUP + 1:
                lo, hi = lo * cosine - hi * sine, hi * cosine + lo * sine
            both = jnp.concatenate([lo, hi], axis=0).astype(jnp.bfloat16)
            put(to, slice(g * 16, g * 16 + 16), both)
    for i in range(SLOTS):
        base = NZ * 2 * W_ROWS + i * C_ROWS
        rows = from_ref[mine[i] >> 3, base : base + C_ROWS, :]
        to = W_ROWS + i * C_ROWS
        for d in range(NX):
            put(d, slice(to, to + C_ROWS), rows)


def first_kernel(
    place, mine, a_ref, h0, h1, h2, h3, bias_ref, cos_ref, sin_ref, out_ref, wt_ref
):
    def put(d, rows, value):
        out_ref[d, rows, :] = value

    hs = (h0, h1, h2, h3)
    project(place, place[1], mine, a_ref, hs, bias_ref, cos_ref, sin_ref, wt_ref, put)


def second_kernel(
    place, mine, b_ref, h0, h1, h2, h3, bias_ref, cos_ref, sin_ref, part_ref, out_ref, wt_ref
):
    c = place[1]

    def put(d, rows, value):
        out_ref[d, 1 - c, rows, :] = value

    hs = (h0, h1, h2, h3)
    project(place, 1 - c, mine, b_ref, hs, bias_ref, cos_ref, sin_ref, wt_ref, put)
    for d in range(NX):
        out_ref[d, c] = part_ref[d]


def attend_kernel(g_ref, live_ref, out_ref, q_ref, kn_ref, vn_ref, kc_ref, vc_ref):
    for x in range(NX):
        for g in range(HEADS):
            pair = [g_ref[x, c, g * 16 : g * 16 + 16, :].astype(jnp.float32) for c in range(NC)]
            for half in range(2):
                rows = jnp.concatenate([p[half * 8 : half * 8 + 8] for p in pair], axis=0)
                rows = rows.astype(jnp.bfloat16)
                at = slice(half * 64 + x * 16, half * 64 + x * 16 + 16)
                if g < GROUP:
                    q_ref[at, g * 128 : (g + 1) * 128] = rows
                elif g == GROUP:
                    kn_ref[at, :] = rows
                else:
                    vn_ref[at, :] = rows
        for k in range(NC):
            for i in range(SLOTS):
                base = W_ROWS + i * C_ROWS
                at = slice((x * NC + k) * TOK, (x * NC + k + 1) * TOK)
                kc_ref[i, at, :] = g_ref[x, k, base : base + TOK, :]
                vc_ref[i, at, :] = g_ref[x, k, base + TOK : base + 2 * TOK, :]
    q = q_ref[...]
    scaling = HD ** (-0.5)
    lane = lax.broadcasted_iota(jnp.int32, (1, GROUP * ROWS), 1) & (ROWS - 1)
    second = lane >= ROWS // 2

    def plain(a, b):
        return jnp.dot(a, b, preferred_element_type=jnp.float32)

    def turned(a, b):
        return lax.dot_general(a, b, (((0,), (0,)), ((), ())), preferred_element_type=jnp.float32)

    scores = jnp.where(second, plain(kc_ref[1], q), plain(kc_ref[0], q)) * scaling
    own = turned(kn_ref[...], q) * scaling
    token = lax.broadcasted_iota(jnp.int32, (ROWS, GROUP * ROWS), 0)
    seen = ((token >> 2) == (lane >> 2)) & ((token & 3) <= (lane & 3))
    own = jnp.where(seen, own, -jnp.inf)
    row_max = jnp.maximum(
        jnp.max(scores, axis=0, keepdims=True), jnp.max(own, axis=0, keepdims=True)
    )
    prompt_exp = jnp.exp(scores - row_max)
    own_exp = jnp.exp(own - row_max)
    total = jnp.sum(prompt_exp, axis=0, keepdims=True) + jnp.sum(own_exp, axis=0, keepdims=True)
    weights = prompt_exp.astype(jnp.bfloat16)
    out = jnp.where(second, turned(vc_ref[1], weights), turned(vc_ref[0], weights))
    out = out + plain(vn_ref[...], own_exp.astype(jnp.bfloat16))
    out = out / total
    for h in range(GROUP):
        part = out[:, h * 128 : (h + 1) * 128]
        part = jnp.where(live_ref[...] > 0, part, 0.0)
        out_ref[:, h * 128 : (h + 1) * 128] = part.T.astype(jnp.bfloat16)


def tables():
    inverse = 1000000.0 ** (-2.0 * np.arange(64) / HD)
    step = np.arange(ROWS) % STEPS
    angles = (PLEN + step)[None, :] * inverse[:, None]
    return np.cos(angles).astype(np.float32), np.sin(angles).astype(np.float32)


def call(kernel, shape, specs, dtype=jnp.bfloat16, scratch=(), flops=0, moved=0, limit=8):
    return pl.pallas_call(
        kernel,
        out_shape=jax.ShapeDtypeStruct(shape, dtype),
        in_specs=specs,
        out_specs=vmem(),
        scratch_shapes=list(scratch),
        cost_estimate=pl.CostEstimate(flops=flops, bytes_accessed=moved, transcendentals=0),
        compiler_params=pltpu.CompilerParams(vmem_limit_bytes=limit * 2**20),
        interpret=INTERPRET,
    )


def hop(array, axis, size, by):
    return lax.ppermute(array, axis, [(i, (i + by) % size) for i in range(size)])


def step(hidden, qkv_weight, qkv_bias, prompt_pool, block_table, group_prompts, decode_len):
    bf16 = jnp.bfloat16
    x = lax.axis_index("x").astype(jnp.int32)
    c = lax.axis_index("c").astype(jnp.int32)
    place = jnp.stack([x, c])

    h0 = hidden.reshape(ROWS, WIDTH)
    h1 = hop(h0, "x", NX, 1)
    h2 = hop(h0, "x", NX, -1)
    h3 = hop(h0, "x", NX, 2)
    wanted = jnp.broadcast_to(group_prompts[None], (NY, SLOTS))
    wanted = lax.all_to_all(wanted, "y", 0, 0, tiled=True)

    sent = call(
        prep_kernel, (Z_ROWS, 128), [smem(), smem(), vmem(), vmem()], moved=600000
    )(
        place,
        block_table,
        qkv_weight.reshape(K_SHARD, HEADS * HD),
        prompt_pool.reshape(SLOTS, 6, 16, 2 * HD),
    )
    zg = lax.all_gather(sent, "zh", axis=0, tiled=True)
    zg = zg.reshape(NZ, Z_ROWS, 128)
    picked = call(pick_kernel, (NY, Y_ROWS, 128), [smem(), vmem()], moved=1500000)(wanted, zg)
    a = lax.all_to_all(picked, "y", 0, 0, tiled=True)
    b = hop(a, "c", NC, 1)

    bias = lax.dynamic_index_in_dim(
        qkv_bias.reshape(HEADS * 2, NX, NC, 8), x, 1, keepdims=False
    )
    bias = bias.transpose(1, 0, 2).reshape(NC, W_ROWS, 1)
    bias = jnp.broadcast_to(bias, (NC, W_ROWS, ROWS))
    cosine, sine = tables()
    cosine, sine = jnp.asarray(cosine), jnp.asarray(sine)
    scratch = [pltpu.VMEM((W_ROWS, WIDTH), bf16)]
    flops = 2 * W_ROWS * WIDTH * 4 * ROWS
    part = call(
        first_kernel,
        (NX, X_ROWS, 128),
        [smem(), smem()] + [vmem()] * 8,
        scratch=scratch,
        flops=flops,
        moved=5500000,
        limit=16,
    )(place, group_prompts, a, h0, h1, h2, h3, bias, cosine, sine)
    made = call(
        second_kernel,
        (NX, NC, X_ROWS, 128),
        [smem(), smem()] + [vmem()] * 9,
        scratch=scratch,
        flops=flops,
        moved=6500000,
        limit=16,
    )(place, group_prompts, b, h0, h1, h2, h3, bias, cosine, sine, part)
    got = lax.all_to_all(made, "x", 0, 0, tiled=True)

    step = jnp.arange(STEPS, dtype=jnp.int32)
    live = (step[None, None, :] < decode_len[:, :, None]).astype(jnp.float32).reshape(1, ROWS)
    out = call(
        attend_kernel,
        (ROWS, GROUP * HD),
        [vmem(), vmem()],
        scratch=[
            pltpu.VMEM((HD, GROUP * ROWS), bf16),
            pltpu.VMEM((HD, ROWS), bf16),
            pltpu.VMEM((HD, ROWS), bf16),
            pltpu.VMEM((SLOTS, PLEN, HD), bf16),
            pltpu.VMEM((SLOTS, PLEN, HD), bf16),
        ],
        flops=400000000,
        moved=1000000,
        limit=16,
    )(got, live)
    return out.reshape(SLOTS, SAMPLES_DEV, STEPS, 1, GROUP * HD)


def solution(mesh):
    names = ("y", "zh", "x", "c", "tp")
    fine = Mesh(mesh.devices.reshape(NY, NZ, NX, NC, mesh.shape["tp"]), names)
    fsdp, sample = ("y", "zh"), ("x", "c")
    return jax.shard_map(
        step,
        mesh=fine,
        in_specs=(
            P(fsdp, sample, None, None),
            P(fsdp, "tp", None),
            P("tp", None),
            P(fsdp, sample, None, "tp", None),
            P(fsdp, sample),
            P(fsdp),
            P(fsdp, sample),
        ),
        out_specs=P(fsdp, sample, None, "tp", None),
        check_vma=False,
    )
```

```python
import jax
import jax.numpy as jnp
import numpy as np
from jax import lax
from jax.experimental import pallas as pl
from jax.experimental.pallas import tpu as pltpu
from jax.sharding import Mesh, PartitionSpec as P


HD = 128
HEADS = 6
GROUP = 4
NY, NZ, NX, NC = 4, 4, 4, 2
SLOTS = 2
SAMPLES_DEV = 16
STEPS = 4
ROWS = SLOTS * SAMPLES_DEV * STEPS
WIDTH = 4096
K_SHARD = 256
W_ROWS = HEADS * HD // (NX * NC)
TOK = 64
C_ROWS = 2 * TOK
Z_ROWS = 2 * W_ROWS + SLOTS * C_ROWS
Y_ROWS = NZ * 2 * W_ROWS + SLOTS * C_ROWS
X_ROWS = W_ROWS + SLOTS * C_ROWS
PLEN = 512
INTERPRET = False


def vmem():
    return pl.BlockSpec(memory_space=pltpu.VMEM)


def smem():
    return pl.BlockSpec(memory_space=pltpu.SMEM)


def prep_kernel(place, table, w_ref, pool_ref, out_ref):
    wt = w_ref[...].T
    for k in range(NX * NC):

        @pl.when(place[0] * NC + place[1] == k)
        def _(k=k):
            for g in range(HEADS * 2):
                lo = g * 64 + k * 8
                for half in range(2):
                    out_ref[0, half * W_ROWS + g * 8 : half * W_ROWS + (g + 1) * 8, :] = wt[
                        lo : lo + 8, half * 128 : (half + 1) * 128
                    ]

    for i in range(SLOTS):
        for b in range(4):
            block = pool_ref[i, table[i, b]]
            base = 2 * W_ROWS + i * C_ROWS + b * 16
            out_ref[0, base : base + 16, :] = block[:, :HD]
            out_ref[0, base + TOK : base + TOK + 16, :] = block[:, HD:]
    for d in range(1, NZ):
        out_ref[d] = out_ref[0]


def pick_kernel(place, w0, w1, w2, w3, zg_ref, out_ref):
    for back, wanted in enumerate((w0, w1, w2, w3)):
        d = (place[2] - back) & 3
        for z in range(NZ):
            out_ref[d, z * 2 * W_ROWS : (z + 1) * 2 * W_ROWS, :] = zg_ref[z, : 2 * W_ROWS, :]
        for i in range(SLOTS):
            p = wanted[i] & 7
            src = pl.ds(pl.multiple_of(2 * W_ROWS + (p & 1) * C_ROWS, 64), C_ROWS)
            base = NZ * 2 * W_ROWS + i * C_ROWS
            out_ref[d, base : base + C_ROWS, :] = zg_ref[p >> 1, src, :]


def project(place, core, mine, from_ref, h_refs, bias_ref, cos_ref, sin_ref, wt_ref, put):
    for y in range(NY):
        for z in range(NZ):
            for half in range(2):
                lo = ((y * NZ + z) * 2 + half) * 128
                wt_ref[:, lo : lo + 128] = from_ref[
                    y, (z * 2 + half) * W_ROWS : (z * 2 + half + 1) * W_ROWS, :
                ]
    at = pl.ds(pl.multiple_of(place[0] * 16 + core * 8, 8), 8)
    cosine = cos_ref[at, :]
    sine = sin_ref[at, :]
    bias = bias_ref[core]
    for h_ref, shift in zip(h_refs, (0, 3, 1, 2)):
        mixed = lax.dot_general(
            wt_ref[...], h_ref[...], (((1,), (1,)), ((), ())), preferred_element_type=jnp.float32
        )
        mixed = mixed + bias
        to = (place[0] + shift) & 3
        for g in range(HEADS):
            lo = mixed[g * 16 : g * 16 + 8]
            hi = mixed[g * 16 + 8 : g * 16 + 16]
            if g < GROUP + 1:
                lo, hi = lo * cosine - hi * sine, hi * cosine + lo * sine
            both = jnp.concatenate([lo, hi], axis=0).astype(jnp.bfloat16)
            put(to, slice(g * 16, g * 16 + 16), both)
    for i in range(SLOTS):
        base = NZ * 2 * W_ROWS + i * C_ROWS
        rows = from_ref[mine[i] >> 3, base : base + C_ROWS, :]
        to = W_ROWS + i * C_ROWS
        for d in range(NX):
            put(d, slice(to, to + C_ROWS), rows)


def first_kernel(
    place, mine, a_ref, h0, h1, h2, h3, bias_ref, cos_ref, sin_ref, out_ref, wt_ref
):
    def put(d, rows, value):
        out_ref[d, rows, :] = value

    hs = (h0, h1, h2, h3)
    project(place, place[1], mine, a_ref, hs, bias_ref, cos_ref, sin_ref, wt_ref, put)


def second_kernel(
    place, mine, b_ref, h0, h1, h2, h3, bias_ref, cos_ref, sin_ref, part_ref, out_ref, wt_ref
):
    c = place[1]

    def put(d, rows, value):
        out_ref[d, 1 - c, rows, :] = value

    hs = (h0, h1, h2, h3)
    project(place, 1 - c, mine, b_ref, hs, bias_ref, cos_ref, sin_ref, wt_ref, put)
    for d in range(NX):
        out_ref[d, c] = part_ref[d]


def attend_kernel(g_ref, live_ref, out_ref, q_ref, kn_ref, vn_ref, kc_ref, vc_ref):
    for x in range(NX):
        for g in range(HEADS):
            pair = [g_ref[x, c, g * 16 : g * 16 + 16, :].astype(jnp.float32) for c in range(NC)]
            for half in range(2):
                rows = jnp.concatenate([p[half * 8 : half * 8 + 8] for p in pair], axis=0)
                rows = rows.astype(jnp.bfloat16)
                at = slice(half * 64 + x * 16, half * 64 + x * 16 + 16)
                if g < GROUP:
                    q_ref[at, g * 128 : (g + 1) * 128] = rows
                elif g == GROUP:
                    kn_ref[at, :] = rows
                else:
                    vn_ref[at, :] = rows
        for k in range(NC):
            for i in range(SLOTS):
                base = W_ROWS + i * C_ROWS
                at = slice((x * NC + k) * TOK, (x * NC + k + 1) * TOK)
                kc_ref[i, at, :] = g_ref[x, k, base : base + TOK, :]
                vc_ref[i, at, :] = g_ref[x, k, base + TOK : base + 2 * TOK, :]
    q = q_ref[...]
    scaling = HD ** (-0.5)
    lane = lax.broadcasted_iota(jnp.int32, (1, GROUP * ROWS), 1) & (ROWS - 1)
    second = lane >= ROWS // 2

    def plain(a, b):
        return jnp.dot(a, b, preferred_element_type=jnp.float32)

    def turned(a, b):
        return lax.dot_general(a, b, (((0,), (0,)), ((), ())), preferred_element_type=jnp.float32)

    scores = jnp.where(second, plain(kc_ref[1], q), plain(kc_ref[0], q)) * scaling
    own = turned(kn_ref[...], q) * scaling
    token = lax.broadcasted_iota(jnp.int32, (ROWS, GROUP * ROWS), 0)
    seen = ((token >> 2) == (lane >> 2)) & ((token & 3) <= (lane & 3))
    own = jnp.where(seen, own, -jnp.inf)
    row_max = jnp.maximum(
        jnp.max(scores, axis=0, keepdims=True), jnp.max(own, axis=0, keepdims=True)
    )
    prompt_exp = jnp.exp(scores - row_max)
    own_exp = jnp.exp(own - row_max)
    total = jnp.sum(prompt_exp, axis=0, keepdims=True) + jnp.sum(own_exp, axis=0, keepdims=True)
    weights = prompt_exp.astype(jnp.bfloat16)
    out = jnp.where(second, turned(vc_ref[1], weights), turned(vc_ref[0], weights))
    out = out + plain(vn_ref[...], own_exp.astype(jnp.bfloat16))
    out = out / total
    for h in range(GROUP):
        part = out[:, h * 128 : (h + 1) * 128]
        part = jnp.where(live_ref[...] > 0, part, 0.0)
        out_ref[:, h * 128 : (h + 1) * 128] = part.T.astype(jnp.bfloat16)


def tables():
    inverse = 1000000.0 ** (-2.0 * np.arange(64) / HD)
    step = np.arange(ROWS) % STEPS
    angles = (PLEN + step)[None, :] * inverse[:, None]
    return np.cos(angles).astype(np.float32), np.sin(angles).astype(np.float32)


def call(kernel, shape, specs, dtype=jnp.bfloat16, scratch=(), flops=0, moved=0, limit=8):
    return pl.pallas_call(
        kernel,
        out_shape=jax.ShapeDtypeStruct(shape, dtype),
        in_specs=specs,
        out_specs=vmem(),
        scratch_shapes=list(scratch),
        cost_estimate=pl.CostEstimate(flops=flops, bytes_accessed=moved, transcendentals=0),
        compiler_params=pltpu.CompilerParams(vmem_limit_bytes=limit * 2**20),
        interpret=INTERPRET,
    )


def hop(array, axis, size, by):
    return lax.ppermute(array, axis, [(i, (i + by) % size) for i in range(size)])


def step(hidden, qkv_weight, qkv_bias, prompt_pool, block_table, group_prompts, decode_len):
    bf16 = jnp.bfloat16
    x = lax.axis_index("x").astype(jnp.int32)
    c = lax.axis_index("c").astype(jnp.int32)
    y = lax.axis_index("y").astype(jnp.int32)
    place = jnp.stack([x, c, y])

    h0 = hidden.reshape(ROWS, WIDTH)
    h1 = hop(h0, "x", NX, 1)
    h2 = hop(h0, "x", NX, -1)
    h3 = hop(h0, "x", NX, 2)
    wanted = [group_prompts]
    for by in range(1, NY):
        wanted.append(hop(group_prompts, "y", NY, by))

    sent = call(
        prep_kernel, (NZ, Z_ROWS, 128), [smem(), smem(), vmem(), vmem()], moved=600000
    )(
        place,
        block_table,
        qkv_weight.reshape(K_SHARD, HEADS * HD),
        prompt_pool.reshape(SLOTS, 6, 16, 2 * HD),
    )
    zg = lax.all_to_all(sent, "zh", 0, 0, tiled=True)
    picked = call(pick_kernel, (NY, Y_ROWS, 128), [smem()] * 5 + [vmem()], moved=1500000)(
        place, *wanted, zg
    )
    a = lax.all_to_all(picked, "y", 0, 0, tiled=True)
    b = hop(a, "c", NC, 1)

    bias = lax.dynamic_index_in_dim(
        qkv_bias.reshape(HEADS * 2, NX, NC, 8), x, 1, keepdims=False
    )
    bias = bias.transpose(1, 0, 2).reshape(NC, W_ROWS, 1)
    bias = jnp.broadcast_to(bias, (NC, W_ROWS, ROWS))
    cosine, sine = tables()
    cosine, sine = jnp.asarray(cosine), jnp.asarray(sine)
    scratch = [pltpu.VMEM((W_ROWS, WIDTH), bf16)]
    flops = 2 * W_ROWS * WIDTH * 4 * ROWS
    part = call(
        first_kernel,
        (NX, X_ROWS, 128),
        [smem(), smem()] + [vmem()] * 8,
        scratch=scratch,
        flops=flops,
        moved=5500000,
        limit=16,
    )(place, group_prompts, a, h0, h1, h2, h3, bias, cosine, sine)
    made = call(
        second_kernel,
        (NX, NC, X_ROWS, 128),
        [smem(), smem()] + [vmem()] * 9,
        scratch=scratch,
        flops=flops,
        moved=6500000,
        limit=16,
    )(place, group_prompts, b, h0, h1, h2, h3, bias, cosine, sine, part)
    got = lax.all_to_all(made, "x", 0, 0, tiled=True)

    step = jnp.arange(STEPS, dtype=jnp.int32)
    live = (step[None, None, :] < decode_len[:, :, None]).astype(jnp.float32).reshape(1, ROWS)
    out = call(
        attend_kernel,
        (ROWS, GROUP * HD),
        [vmem(), vmem()],
        scratch=[
            pltpu.VMEM((HD, GROUP * ROWS), bf16),
            pltpu.VMEM((HD, ROWS), bf16),
            pltpu.VMEM((HD, ROWS), bf16),
            pltpu.VMEM((SLOTS, PLEN, HD), bf16),
            pltpu.VMEM((SLOTS, PLEN, HD), bf16),
        ],
        flops=400000000,
        moved=1000000,
        limit=16,
    )(got, live)
    return out.reshape(SLOTS, SAMPLES_DEV, STEPS, 1, GROUP * HD)


def solution(mesh):
    names = ("y", "zh", "x", "c", "tp")
    fine = Mesh(mesh.devices.reshape(NY, NZ, NX, NC, mesh.shape["tp"]), names)
    fsdp, sample = ("y", "zh"), ("x", "c")
    return jax.shard_map(
        step,
        mesh=fine,
        in_specs=(
            P(fsdp, sample, None, None),
            P(fsdp, "tp", None),
            P("tp", None),
            P(fsdp, sample, None, "tp", None),
            P(fsdp, sample),
            P(fsdp),
            P(fsdp, sample),
        ),
        out_specs=P(fsdp, sample, None, "tp", None),
        check_vma=False,
    )
```

```python
import jax
import jax.numpy as jnp
import numpy as np
from jax import lax
from jax.experimental import pallas as pl
from jax.experimental.pallas import tpu as pltpu
from jax.sharding import Mesh, PartitionSpec as P


HD = 128
HEADS = 6
GROUP = 4
NY, NZ, NX, NC = 4, 4, 4, 2
SLOTS = 2
SAMPLES_DEV = 16
STEPS = 4
ROWS = SLOTS * SAMPLES_DEV * STEPS
WIDTH = 4096
K_SHARD = 256
W_ROWS = HEADS * HD // (NX * NC)
TOK = 64
C_ROWS = 2 * TOK
Z_ROWS = 2 * W_ROWS + SLOTS * C_ROWS
Y_ROWS = NZ * 2 * W_ROWS + SLOTS * C_ROWS
X_ROWS = W_ROWS + SLOTS * C_ROWS
PLEN = 512
INTERPRET = False


def vmem():
    return pl.BlockSpec(memory_space=pltpu.VMEM)


def smem():
    return pl.BlockSpec(memory_space=pltpu.SMEM)


def prep_kernel(place, table, w_ref, pool_ref, out_ref):
    wt = w_ref[...].T
    for k in range(NX * NC):

        @pl.when(place[0] * NC + place[1] == k)
        def _(k=k):
            for g in range(HEADS * 2):
                lo = g * 64 + k * 8
                for half in range(2):
                    out_ref[half * W_ROWS + g * 8 : half * W_ROWS + (g + 1) * 8, :] = wt[
                        lo : lo + 8, half * 128 : (half + 1) * 128
                    ]

    for i in range(SLOTS):
        for b in range(4):
            block = pool_ref[i, table[i, b]]
            base = 2 * W_ROWS + i * C_ROWS + b * 16
            out_ref[base : base + 16, :] = block[:, :HD]
            out_ref[base + TOK : base + TOK + 16, :] = block[:, HD:]


def pick_kernel(wanted, zg_ref, out_ref):
    for d in range(NY):
        for z in range(NZ):
            out_ref[d, z * 2 * W_ROWS : (z + 1) * 2 * W_ROWS, :] = zg_ref[z, : 2 * W_ROWS, :]
        for i in range(SLOTS):
            p = wanted[d, i] & 7
            src = pl.ds(pl.multiple_of(2 * W_ROWS + (p & 1) * C_ROWS, 64), C_ROWS)
            base = NZ * 2 * W_ROWS + i * C_ROWS
            out_ref[d, base : base + C_ROWS, :] = zg_ref[p >> 1, src, :]


def project(place, core, mine, from_ref, h_ref, bias_ref, cos_ref, sin_ref, wt_ref, put):
    for y in range(NY):
        for z in range(NZ):
            for half in range(2):
                lo = ((y * NZ + z) * 2 + half) * 128
                wt_ref[:, lo : lo + 128] = from_ref[
                    y, (z * 2 + half) * W_ROWS : (z * 2 + half + 1) * W_ROWS, :
                ]
    at = pl.ds(pl.multiple_of(place[0] * 16 + core * 8, 8), 8)
    cosine = cos_ref[at, :]
    sine = sin_ref[at, :]
    bias = bias_ref[core]
    every = lax.dot_general(
        h_ref[...], wt_ref[...], (((1,), (1,)), ((), ())), preferred_element_type=jnp.float32
    ).T
    for k, shift in enumerate((0, 3, 1, 2)):
        mixed = every[:, k * ROWS : (k + 1) * ROWS] + bias
        to = (place[0] + shift) & 3
        for g in range(HEADS):
            lo = mixed[g * 16 : g * 16 + 8]
            hi = mixed[g * 16 + 8 : g * 16 + 16]
            if g < GROUP + 1:
                lo, hi = lo * cosine - hi * sine, hi * cosine + lo * sine
            both = jnp.concatenate([lo, hi], axis=0).astype(jnp.bfloat16)
            put(to, slice(g * 16, g * 16 + 16), both)
    for i in range(SLOTS):
        base = NZ * 2 * W_ROWS + i * C_ROWS
        rows = from_ref[mine[i] >> 3, base : base + C_ROWS, :]
        to = W_ROWS + i * C_ROWS
        for d in range(NX):
            put(d, slice(to, to + C_ROWS), rows)


def first_kernel(
    place, mine, a_ref, h0, h1, h2, h3, bias_ref, cos_ref, sin_ref, out_ref, h_ref, wt_ref
):
    def put(d, rows, value):
        out_ref[d, rows, :] = value

    for k, ref in enumerate((h0, h1, h2, h3)):
        h_ref[k * ROWS : (k + 1) * ROWS, :] = ref[...]
    project(place, place[1], mine, a_ref, h_ref, bias_ref, cos_ref, sin_ref, wt_ref, put)


def second_kernel(
    place, mine, b_ref, h_ref, bias_ref, cos_ref, sin_ref, part_ref, out_ref, wt_ref
):
    c = place[1]

    def put(d, rows, value):
        out_ref[d, 1 - c, rows, :] = value

    project(place, 1 - c, mine, b_ref, h_ref, bias_ref, cos_ref, sin_ref, wt_ref, put)
    for d in range(NX):
        out_ref[d, c] = part_ref[d]


def attend_kernel(lengths, g_ref, out_ref, q_ref, kn_ref, vn_ref, kc_ref, vc_ref):
    for x in range(NX):
        for g in range(HEADS):
            pair = [g_ref[x, c, g * 16 : g * 16 + 16, :].astype(jnp.float32) for c in range(NC)]
            for half in range(2):
                rows = jnp.concatenate([p[half * 8 : half * 8 + 8] for p in pair], axis=0)
                rows = rows.astype(jnp.bfloat16)
                at = slice(half * 64 + x * 16, half * 64 + x * 16 + 16)
                if g < GROUP:
                    q_ref[at, g * 128 : (g + 1) * 128] = rows
                elif g == GROUP:
                    kn_ref[at, :] = rows
                else:
                    vn_ref[at, :] = rows
        for k in range(NC):
            for i in range(SLOTS):
                base = W_ROWS + i * C_ROWS
                at = slice((x * NC + k) * TOK, (x * NC + k + 1) * TOK)
                kc_ref[i, at, :] = g_ref[x, k, base : base + TOK, :]
                vc_ref[i, at, :] = g_ref[x, k, base + TOK : base + 2 * TOK, :]
    row = lax.broadcasted_iota(jnp.int32, (1, ROWS), 1)
    live = jnp.zeros((1, ROWS), jnp.int32)
    for i in range(SLOTS):
        for k in range(SAMPLES_DEV):
            live = jnp.where((row >> 2) == i * SAMPLES_DEV + k, lengths[i, k], live)
    live = (row & 3) < live
    q = q_ref[...]
    scaling = HD ** (-0.5)
    lane = lax.broadcasted_iota(jnp.int32, (1, GROUP * ROWS), 1) & (ROWS - 1)
    second = lane >= ROWS // 2

    def plain(a, b):
        return jnp.dot(a, b, preferred_element_type=jnp.float32)

    def turned(a, b):
        return lax.dot_general(a, b, (((0,), (0,)), ((), ())), preferred_element_type=jnp.float32)

    scores = jnp.where(second, plain(kc_ref[1], q), plain(kc_ref[0], q)) * scaling
    own = turned(kn_ref[...], q) * scaling
    token = lax.broadcasted_iota(jnp.int32, (ROWS, GROUP * ROWS), 0)
    seen = ((token >> 2) == (lane >> 2)) & ((token & 3) <= (lane & 3))
    own = jnp.where(seen, own, -jnp.inf)
    row_max = jnp.maximum(
        jnp.max(scores, axis=0, keepdims=True), jnp.max(own, axis=0, keepdims=True)
    )
    prompt_exp = jnp.exp(scores - row_max)
    own_exp = jnp.exp(own - row_max)
    total = jnp.sum(prompt_exp, axis=0, keepdims=True) + jnp.sum(own_exp, axis=0, keepdims=True)
    weights = prompt_exp.astype(jnp.bfloat16)
    out = jnp.where(second, turned(vc_ref[1], weights), turned(vc_ref[0], weights))
    out = out + plain(vn_ref[...], own_exp.astype(jnp.bfloat16))
    out = out / total
    for h in range(GROUP):
        part = out[:, h * 128 : (h + 1) * 128]
        part = jnp.where(live, part, 0.0)
        out_ref[:, h * 128 : (h + 1) * 128] = part.T.astype(jnp.bfloat16)


def tables():
    inverse = 1000000.0 ** (-2.0 * np.arange(64) / HD)
    step = np.arange(ROWS) % STEPS
    angles = (PLEN + step)[None, :] * inverse[:, None]
    return np.cos(angles).astype(np.float32), np.sin(angles).astype(np.float32)


def call(kernel, shape, specs, scratch=(), flops=0, moved=0, limit=8):
    many = isinstance(shape, list)
    shapes = [jax.ShapeDtypeStruct(sh, jnp.bfloat16) for sh in (shape if many else [shape])]
    return pl.pallas_call(
        kernel,
        out_shape=shapes if many else shapes[0],
        in_specs=specs,
        out_specs=[vmem()] * len(shapes) if many else vmem(),
        scratch_shapes=list(scratch),
        cost_estimate=pl.CostEstimate(flops=flops, bytes_accessed=moved, transcendentals=0),
        compiler_params=pltpu.CompilerParams(vmem_limit_bytes=limit * 2**20),
        interpret=INTERPRET,
    )


def hop(array, axis, size, by):
    return lax.ppermute(array, axis, [(i, (i + by) % size) for i in range(size)])


def step(hidden, qkv_weight, qkv_bias, prompt_pool, block_table, group_prompts, decode_len):
    bf16 = jnp.bfloat16
    x = lax.axis_index("x").astype(jnp.int32)
    c = lax.axis_index("c").astype(jnp.int32)
    place = jnp.stack([x, c])

    h0 = hidden.reshape(ROWS, WIDTH)
    h1 = hop(h0, "x", NX, 1)
    h2 = hop(h0, "x", NX, -1)
    h3 = hop(h0, "x", NX, 2)
    wanted = jnp.broadcast_to(group_prompts[None], (NY, SLOTS))
    wanted = lax.all_to_all(wanted, "y", 0, 0, tiled=True)

    sent = call(
        prep_kernel, (Z_ROWS, 128), [smem(), smem(), vmem(), vmem()], moved=600000, limit=60
    )(
        place,
        block_table,
        qkv_weight.reshape(K_SHARD, HEADS * HD),
        prompt_pool.reshape(SLOTS, 6, 16, 2 * HD),
    )
    zg = lax.all_gather(sent, "zh", axis=0, tiled=True)
    zg = zg.reshape(NZ, Z_ROWS, 128)
    picked = call(pick_kernel, (NY, Y_ROWS, 128), [smem(), vmem()], moved=1500000)(wanted, zg)
    a = lax.all_to_all(picked, "y", 0, 0, tiled=True)
    b = hop(a, "c", NC, 1)

    bias = lax.dynamic_index_in_dim(
        qkv_bias.reshape(HEADS * 2, NX, NC, 8), x, 1, keepdims=False
    )
    bias = bias.transpose(1, 0, 2).reshape(NC, W_ROWS, 1)
    bias = jnp.broadcast_to(bias, (NC, W_ROWS, ROWS))
    cosine, sine = tables()
    cosine, sine = jnp.asarray(cosine), jnp.asarray(sine)
    scratch = [pltpu.VMEM((W_ROWS, WIDTH), bf16)]
    flops = 2 * W_ROWS * WIDTH * 4 * ROWS
    part, every = call(
        first_kernel,
        [(NX, X_ROWS, 128), (NX * ROWS, WIDTH)],
        [smem(), smem()] + [vmem()] * 8,
        scratch=scratch,
        flops=flops,
        moved=5500000,
        limit=16,
    )(place, group_prompts, a, h0, h1, h2, h3, bias, cosine, sine)
    made = call(
        second_kernel,
        (NX, NC, X_ROWS, 128),
        [smem(), smem()] + [vmem()] * 6,
        scratch=scratch,
        flops=flops,
        moved=6500000,
        limit=16,
    )(place, group_prompts, b, every, bias, cosine, sine, part)
    got = lax.all_to_all(made, "x", 0, 0, tiled=True)

    out = call(
        attend_kernel,
        (ROWS, GROUP * HD),
        [smem(), vmem()],
        scratch=[
            pltpu.VMEM((HD, GROUP * ROWS), bf16),
            pltpu.VMEM((HD, ROWS), bf16),
            pltpu.VMEM((HD, ROWS), bf16),
            pltpu.VMEM((SLOTS, PLEN, HD), bf16),
            pltpu.VMEM((SLOTS, PLEN, HD), bf16),
        ],
        flops=400000000,
        moved=1000000,
        limit=16,
    )(decode_len, got)
    return out.reshape(SLOTS, SAMPLES_DEV, STEPS, 1, GROUP * HD)


def solution(mesh):
    names = ("y", "zh", "x", "c", "tp")
    fine = Mesh(mesh.devices.reshape(NY, NZ, NX, NC, mesh.shape["tp"]), names)
    fsdp, sample = ("y", "zh"), ("x", "c")
    return jax.shard_map(
        step,
        mesh=fine,
        in_specs=(
            P(fsdp, sample, None, None),
            P(fsdp, "tp", None),
            P("tp", None),
            P(fsdp, sample, None, "tp", None),
            P(fsdp, sample),
            P(fsdp),
            P(fsdp, sample),
        ),
        out_specs=P(fsdp, sample, None, "tp", None),
        check_vma=False,
    )
```
